32 devices in a mesh: rows: 8 (over z, x), col: 4 (over y, core).
Axes of the slice: x: 2, y: 2, z: 4, core: 2. Of those that a mesh axis runs over, the one named last changes fastest.
Arguments:
- factor_t: bfloat16 [112, 128, 128], P('rows', 'col'), may hold values from -0.25 to 1.25
- intersection_diag: bfloat16 [112, 128, 128], P('rows'), may hold values from -0.25 to 1.25
- intersection_near: bfloat16 [112, 3, 128, 128], P('rows'), may hold values from -0.3125 to 0.3125
- intersection_cross: bfloat16 [112, 4, 128, 128], P('rows'), may hold values from -0.3125 to 0.3125
- near_cols: int32 [112, 3], P('rows'), may hold values from 0 to 111, as said below
- cross_cols: int32 [112, 4], P('rows'), may hold values from 0 to 111, as said below
Outputs:
- refined_diag: bfloat16 [112, 128, 128], P('rows', 'col')
- refined_near: bfloat16 [112, 3, 128, 128], P('rows', None, 'col')
- refined_cross: bfloat16 [112, 4, 128, 128], P('rows', None, 'col')
The draws below stay inside these ranges and needn't reach their ends.
Inputs may be any that keep to these rules, and one draw needn't show every extreme that they name: near_cols[i, k] differs from i by 1 to 14. cross_cols[i, k] lies in the other half of the block rows; the block rows i * 14 to i * 14 + 13 name at most 14 columns in any one group of 14 block rows, and some group is named that often.
All inputs are finite; a program needn't handle non-finite values.
Results may differ from the reference program's by a relative error of at most 0.0056.
Values may be sent and summed in bfloat16 or wider, within the bound.
A program may use at most 64 MiB of HBM per device.

```python
import jax
import jax.numpy as jnp
from jax import lax

B = 128
NEAR = 3
CROSS = 4
ROW_BLOCKS_EACH = 14
NB = 112
HALFDEV = 4
CAP = 14


def draw_factor_t(key, part):
    scale_value = 0.3 / B ** 0.5
    jitter = jax.random.normal(key, (NB, B, B), jnp.float32) * scale_value
    jitter = jnp.clip(jitter, -0.2, 0.2)
    return (jnp.eye(B, dtype=jnp.float32)[None] + jitter).astype(jnp.bfloat16)


def draw_intersection_diag(key, part):
    scale_value = 0.3 / B ** 0.5
    jitter = jax.random.normal(key, (NB, B, B), jnp.float32) * scale_value
    symmetric = jnp.clip((jitter + jnp.swapaxes(jitter, 1, 2)) * 0.7071, -0.2, 0.2)
    return (jnp.eye(B, dtype=jnp.float32)[None] + symmetric).astype(jnp.bfloat16)


def draw_near_cols(key, part):
    key_offset, key_sign = jax.random.split(jax.random.fold_in(key, 11))
    row_ids = jnp.arange(NB, dtype=jnp.int32)[:, None]
    offsets = jax.random.randint(key_offset, (NB, NEAR), 1, ROW_BLOCKS_EACH + 1)
    random_sign = jax.random.randint(key_sign, (NB, NEAR), 0, 2) * 2 - 1
    fixed_sign = jnp.where(jnp.arange(NEAR)[None, :] == 0, 1, -1)
    direction = jnp.where(jnp.arange(NEAR)[None, :] < 2, fixed_sign, random_sign)
    candidate = row_ids + direction * offsets
    outside = (candidate < 0) | (candidate >= NB)
    return jnp.where(outside, row_ids - direction * offsets, candidate).astype(jnp.int32)


def draw_cross_cols(key, part):
    key_perm, key_row = jax.random.split(jax.random.fold_in(key, 23))
    devices = NB // ROW_BLOCKS_EACH
    slots = ROW_BLOCKS_EACH * CROSS
    device_keys = jax.random.split(key_perm, devices)
    chosen = jax.vmap(lambda subkey: jax.random.permutation(subkey, HALFDEV * CAP)[:slots])(device_keys) // CAP
    device_ids = jnp.arange(devices, dtype=jnp.int32)[:, None]
    target = chosen + jnp.where(device_ids < HALFDEV, HALFDEV, 0)
    inside_range = jax.random.randint(key_row, (devices, slots), 0, ROW_BLOCKS_EACH)
    return (target * ROW_BLOCKS_EACH + inside_range).reshape(NB, CROSS).astype(jnp.int32)


def levels(stream_key, dims, cuts, least, largest):
    def one(position, parts):
        draws = jax.random.uniform(jax.random.fold_in(jax.random.fold_in(stream_key, 6), position), (parts,), jnp.float32, least / len(cuts), largest / len(cuts))
        return jnp.repeat(jnp.exp(draws), dims[position] // parts).reshape((-1,) + (1,) * (len(dims) - position - 1))

    level = one(*cuts[0])
    for cut in cuts[1:]:
        level = level * one(*cut)
    return level


def bell_draw(own_key, extent, spread, bound, cuts=(), kind=jnp.bfloat16):
    values = spread * jax.random.normal(own_key, extent, jnp.float32)
    if cuts:
        values = values * levels(own_key, extent, cuts, -0.22, 0.18)
    return jnp.clip(values, -bound, bound).astype(kind)


def setup_inputs(seed: int = 0) -> dict:
    splits = jax.random.split(jax.random.key(seed), 7)
    return {
        "factor_t": draw_factor_t(jax.random.fold_in(splits[6], 71), 0),
        "intersection_diag": draw_intersection_diag(jax.random.fold_in(splits[6], 71), 0),
        "intersection_near": bell_draw(splits[2], (NB, NEAR, B, B), (3 * B) ** -0.5, 0.3125, ((0, 8),)),
        "intersection_cross": bell_draw(splits[3], (NB, CROSS, B, B), (3 * B) ** -0.5, 0.3125, ((0, 8),)),
        "near_cols": draw_near_cols(jax.random.fold_in(splits[6], 71), 0),
        "cross_cols": draw_cross_cols(jax.random.fold_in(splits[6], 71), 0),
    }


def refine_row(local_full_rows, others, blocks, eye_part, diagonal_part):
    product = jnp.einsum("kcb,kab->kca", others, blocks.astype(jnp.float32))
    product = lax.optimization_barrier(product.astype(jnp.bfloat16)).astype(jnp.float32)
    quadratic = jnp.einsum("kca,da->kcd", product, local_full_rows)
    residual_error = lax.optimization_barrier((eye_part - quadratic).astype(jnp.bfloat16)).astype(jnp.float32)
    correction_step = jnp.einsum("kca,ad->kcd", residual_error, local_full_rows)
    return (diagonal_part + 0.5 * correction_step).astype(jnp.bfloat16)


def reference(factor_t, intersection_diag, intersection_near, intersection_cross, near_cols, cross_cols):
    whole = factor_t.astype(jnp.float32)
    identity = jnp.eye(B, dtype=jnp.float32)

    def one_row(items):
        own_block, diagonal_block_matrix, near_blocks, cross_blocks, near_index, cross_index = items
        local_full_rows = own_block.astype(jnp.float32)
        diag_out = refine_row(local_full_rows, local_full_rows[None], diagonal_block_matrix[None], identity, local_full_rows[None])[0]
        near_out = refine_row(local_full_rows, whole[near_index], near_blocks, jnp.float32(0.0), jnp.float32(0.0))
        cross_out = refine_row(local_full_rows, whole[cross_index], cross_blocks, jnp.float32(0.0), jnp.float32(0.0))
        return diag_out, near_out, cross_out

    refined_diag, refined_near, refined_cross = lax.map(one_row, (factor_t, intersection_diag, intersection_near, intersection_cross, near_cols, cross_cols))
    return refined_diag, refined_near, refined_cross
```

```python
import functools

import jax
import jax.numpy as jnp
from jax import lax
from jax.experimental import pallas as pl
from jax.experimental.pallas import tpu as pltpu
from jax.sharding import PartitionSpec as P

F32 = jnp.float32
BF16 = jnp.bfloat16
NT = (((1,), (1,)), ((), ()))
TN = (((0,), (0,)), ((), ()))


def dot(a, b, dims=(((1,), (0,)), ((), ()))):
    return lax.dot_general(a, b, dims, preferred_element_type=F32)


def kernel(
    n, c, parts,
    near_cols, cross_cols, factor, s_diag, s_near, s_cross,
    o_diag, o_near, o_cross,
    everyone, full, v_diag, v_near, v_cross, g, w_diag, w_near, w_cross,
    load_sem, own_sem, out_sem, col_send, col_recv, near_send, near_recv,
    first_send, slot_recv, second_send, third_send,
):
    per, width, order = factor.shape
    near, cross = v_near.shape[1], v_cross.shape[1]
    half = n // 2
    piece = per // parts
    r = lax.axis_index("rows")
    q = lax.axis_index("col")
    upper = r // half
    m = r - upper * half
    my_base = upper * half
    other_base = (1 - upper) * half
    parity = m % 2
    mate = my_base + m + 1 - 2 * parity
    side = m - 1 + 2 * parity
    has_side = jnp.logical_and(side >= 0, side < half)
    partner = other_base + m
    cousins = [my_base + (m + 2 * k) % half for k in range(1, half // 2)]
    columns = [(q + k) % c for k in range(1, c)]

    loads = [
        pltpu.make_async_copy(s_diag, v_diag, load_sem.at[0]),
        pltpu.make_async_copy(s_near, v_near, load_sem.at[1]),
        pltpu.make_async_copy(s_cross, v_cross, load_sem.at[2]),
    ]
    own_all = pltpu.make_async_copy(factor, everyone.at[pl.ds(r * per, per)], own_sem.at[0])
    my_rows = pl.ds(pl.multiple_of(q * width, width), width)
    own_full = pltpu.make_async_copy(factor, full.at[:, my_rows, :], own_sem.at[1])

    barrier = pltpu.get_barrier_semaphore()

    def greet(**where):
        pl.semaphore_signal(barrier, inc=1, device_id=where, device_id_type=pl.DeviceIdType.MESH)

    greet(rows=partner)
    greet(rows=mate)
    for cousin in cousins:
        greet(rows=cousin)
    for column in columns:
        greet(col=column)

    @pl.when(has_side)
    def _():
        greet(rows=my_base + side)

    own_full.start()
    own_all.start()
    for load in loads:
        load.start()
    pl.semaphore_wait(barrier, 2 + len(cousins) + len(columns) + has_side.astype(jnp.int32))

    def send(src, dst, send_sem, recv_sem, **where):
        return pltpu.make_async_remote_copy(
            src_ref=src, dst_ref=dst, send_sem=send_sem, recv_sem=recv_sem,
            device_id=where, device_id_type=pl.DeviceIdType.MESH,
        )

    firsts = []
    for p in range(parts):
        firsts.append(send(
            factor.at[pl.ds(p * piece, piece)],
            everyone.at[pl.ds(r * per + p * piece, piece)],
            first_send.at[p], slot_recv.at[m, p], rows=partner,
        ))
        firsts[-1].start()
    cols = []
    for k, column in enumerate(columns):
        cols.append(send(
            factor, full.at[:, my_rows, :], col_send.at[k], col_recv.at[k], col=column,
        ))
        cols[-1].start()
    mine = everyone.at[pl.ds(r * per, per)]
    to_mate = send(factor, mine, near_send.at[0], near_recv.at[0], rows=mate)
    to_mate.start()
    to_side = send(factor, mine, near_send.at[1], near_recv.at[1], rows=my_base + side)

    @pl.when(has_side)
    def _():
        to_side.start()

    def slot(s, p):
        return everyone.at[pl.ds((other_base + s) * per + p * piece, piece)]

    def arrived(s, p):
        return send(slot(s, p), slot(s, p), first_send.at[p], slot_recv.at[s, p], rows=mate)

    sent = []

    def pass_on(s, p, send_sem, row):
        copy = send(slot(s, p), slot(s, p), send_sem, slot_recv.at[s, p], rows=row)
        copy.start()
        sent.append(copy)

    for p in range(parts):
        arrived(m, p).wait_recv()
        for k, cousin in enumerate(cousins):
            pass_on(m, p, second_send.at[k, p], cousin)
        pass_on(m, p, third_send.at[0, p], mate)

    own_full.wait()
    for load in loads:
        load.wait()
    for copy in cols:
        copy.wait_recv()

    eye = (
        lax.broadcasted_iota(jnp.int32, (width, order), 0) + q * width
        == lax.broadcasted_iota(jnp.int32, (width, order), 1)
    ).astype(F32)

    def prepare(i, carry):
        z_t = full[i]
        own = full[i, my_rows, :]
        square = (-0.5 * dot(z_t, z_t, TN)).astype(BF16)
        blocks = [v_near[i, k] for k in range(near)] + [v_cross[i, k] for k in range(cross)]
        wide = dot(square, jnp.concatenate(blocks, axis=1)).astype(BF16)
        for k in range(near + cross):
            g[i, k] = wide[:, k * order:(k + 1) * order]
        product = dot(own, v_diag[i], NT).astype(BF16)
        residual = (eye - dot(product, z_t, NT)).astype(BF16)
        w_diag[i] = (own.astype(F32) + 0.5 * dot(residual, z_t)).astype(BF16)
        return carry

    lax.fori_loop(0, per // 2, prepare, 0)
    for p in range(parts):
        for k in range(1, half // 2):
            s = (m + 2 * k) % half
            arrived(s, p).wait_recv()
            pass_on(s, p, third_send.at[k, p], mate)
    lax.fori_loop(per // 2, per, prepare, 0)
    out_diag = pltpu.make_async_copy(w_diag, o_diag, out_sem.at[2, 0])
    out_diag.start()

    own_all.wait()
    to_mate.wait_recv()

    @pl.when(has_side)
    def _():
        to_side.wait_recv()

    for p in range(parts):
        for k in range(half // 2):
            arrived((m + 1 - 2 * parity + 2 * k) % half, p).wait_recv()

    def outs(i):
        return (
            pltpu.make_async_copy(w_near.at[i], o_near.at[i], out_sem.at[0, i]),
            pltpu.make_async_copy(w_cross.at[i], o_cross.at[i], out_sem.at[1, i]),
        )

    def finish(i, carry):
        for k in range(near):
            w_near[i, k] = dot(everyone[near_cols[k, i]], g[i, k], NT).astype(BF16)
        for k in range(cross):
            w_cross[i, k] = dot(everyone[cross_cols[k, i]], g[i, near + k], NT).astype(BF16)
        for copy in outs(i):
            copy.start()
        return carry

    lax.fori_loop(0, per, finish, 0)

    for copy in firsts + cols + sent + [to_mate]:
        copy.wait_send()

    @pl.when(has_side)
    def _():
        to_side.wait_send()

    out_diag.wait()

    def drain(i, carry):
        for copy in outs(i):
            copy.wait()
        return carry

    lax.fori_loop(0, per, drain, 0)


def body(n, c, factor_t, intersection_diag, intersection_near, intersection_cross, near_cols, cross_cols):
    per, width, order = factor_t.shape
    near, cross = near_cols.shape[1], cross_cols.shape[1]
    half = n // 2
    parts = 2 if per % 2 == 0 else 1
    smem = pl.BlockSpec(memory_space=pltpu.SMEM)
    hbm = pl.BlockSpec(memory_space=pl.ANY)
    dma = pltpu.SemaphoreType.DMA
    return pl.pallas_call(
        functools.partial(kernel, n, c, parts),
        out_shape=(
            jax.ShapeDtypeStruct((per, width, order), BF16),
            jax.ShapeDtypeStruct((per, near, width, order), BF16),
            jax.ShapeDtypeStruct((per, cross, width, order), BF16),
        ),
        in_specs=[smem, smem, hbm, hbm, hbm, hbm],
        out_specs=(hbm, hbm, hbm),
        scratch_shapes=[
            pltpu.VMEM((n * per, width, order), BF16),
            pltpu.VMEM((per, order, order), BF16),
            pltpu.VMEM(intersection_diag.shape, BF16),
            pltpu.VMEM(intersection_near.shape, BF16),
            pltpu.VMEM(intersection_cross.shape, BF16),
            pltpu.VMEM((per, near + cross, order, order), BF16),
            pltpu.VMEM((per, width, order), BF16),
            pltpu.VMEM((per, near, width, order), BF16),
            pltpu.VMEM((per, cross, width, order), BF16),
            dma((3,)),
            dma((2,)),
            dma((3, per)),
            dma((c - 1,)),
            dma((c - 1,)),
            dma((2,)),
            dma((2,)),
            dma((parts,)),
            dma((half, parts)),
            dma((half // 2, parts)),
            dma((half // 2, parts)),
        ],
        compiler_params=pltpu.CompilerParams(collective_id=0, has_side_effects=True),
    )(near_cols.T, cross_cols.T, factor_t, intersection_diag, intersection_near, intersection_cross)


def solution(mesh):
    placed = (
        P("rows", "col", None),
        P("rows", None, None),
        P("rows", None, None, None),
        P("rows", None, None, None),
        P("rows", None),
        P("rows", None),
    )
    return jax.shard_map(
        functools.partial(body, mesh.shape["rows"], mesh.shape["col"]),
        mesh=mesh,
        in_specs=placed,
        out_specs=(
            P("rows", "col", None),
            P("rows", None, "col", None),
            P("rows", None, "col", None),
        ),
        check_vma=False,
    )
```

```python
import functools

import jax
import jax.numpy as jnp
from jax import lax
from jax.experimental import pallas as pl
from jax.experimental.pallas import tpu as pltpu
from jax.sharding import PartitionSpec as P

F32 = jnp.float32
BF16 = jnp.bfloat16
LAG = 3
VMEM_LIMIT = 16 * 1024 * 1024
NT = (((1,), (1,)), ((), ()))
TN = (((0,), (0,)), ((), ()))


def dot(a, b, dims=(((1,), (0,)), ((), ()))):
    return lax.dot_general(a, b, dims, preferred_element_type=F32)


def split(rows, parts):
    size = rows // parts
    return [pl.ds(p * size, size) for p in range(parts)]


def gather_kernel(
    n, c, parts, lag,
    factor, s_diag, s_near, s_cross,
    everyone, g, w_diag,
    full, v_diag, v_near, v_cross,
    load_sem, own_sem, col_send, col_recv, near_send, near_recv,
    first_send, slot_recv, second_send, third_send,
):
    per, width, order = factor.shape
    near, cross = v_near.shape[1], v_cross.shape[1]
    half = n // 2
    piece = per // parts
    r = lax.axis_index("rows")
    q = lax.axis_index("col")
    upper = r // half
    m = r - upper * half
    my_base = upper * half
    other_base = (1 - upper) * half
    parity = m % 2
    mate = my_base + m + 1 - 2 * parity
    side = m - 1 + 2 * parity
    has_side = jnp.logical_and(side >= 0, side < half)
    partner = other_base + m
    cousins = [my_base + (m + 2 * k) % half for k in range(1, half // 2)]
    col_mate = q + 1 - 2 * (q % 2)
    col_cousins = [(q + 2 * k) % c for k in range(1, c // 2)]

    loads = [
        pltpu.make_async_copy(s_diag, v_diag, load_sem.at[0]),
        pltpu.make_async_copy(s_near, v_near, load_sem.at[1]),
        pltpu.make_async_copy(s_cross, v_cross, load_sem.at[2]),
    ]
    own_all = pltpu.make_async_copy(factor, everyone.at[pl.ds(r * per, per)], own_sem.at[0])

    def rows_of(column):
        return pl.ds(pl.multiple_of(column * width, width), width)

    own_full = pltpu.make_async_copy(factor, full.at[:, rows_of(q), :], own_sem.at[1])

    barrier = pltpu.get_barrier_semaphore()

    def greet(**where):
        pl.semaphore_signal(barrier, inc=1, device_id=where, device_id_type=pl.DeviceIdType.MESH)

    greet(rows=partner)
    greet(rows=mate)
    for cousin in cousins:
        greet(rows=cousin)
    greet(col=col_mate)
    for column in col_cousins:
        greet(col=column)

    @pl.when(has_side)
    def _():
        greet(rows=my_base + side)

    own_full.start()
    own_all.start()
    for load in loads:
        load.start()
    pl.semaphore_wait(barrier, 3 + len(cousins) + len(col_cousins) + has_side.astype(jnp.int32))

    def send(src, dst, send_sem, recv_sem, **where):
        return pltpu.make_async_remote_copy(
            src_ref=src, dst_ref=dst, send_sem=send_sem, recv_sem=recv_sem,
            device_id=where, device_id_type=pl.DeviceIdType.MESH,
        )

    sent = []

    def go(*args, **where):
        copy = send(*args, **where)
        copy.start()
        sent.append(copy)
        return copy

    for p in range(parts):
        go(
            factor.at[pl.ds(p * piece, piece)],
            everyone.at[pl.ds(r * per + p * piece, piece)],
            first_send.at[p], slot_recv.at[m, p], rows=partner,
        )
    halves = split(per, col_recv.shape[1])

    def column_piece(column, h):
        return full.at[halves[h], rows_of(column), :]

    for h in range(len(halves)):
        for k, column in enumerate(col_cousins):
            go(factor.at[halves[h]], column_piece(q, h), col_send.at[k, h], col_recv.at[q, h], col=column)
        go(factor.at[halves[h]], column_piece(q, h), col_send.at[len(col_cousins), h], col_recv.at[q, h], col=col_mate)
    mine = everyone.at[pl.ds(r * per, per)]
    to_mate = go(factor, mine, near_send.at[0], near_recv.at[0], rows=mate)
    to_side = send(factor, mine, near_send.at[1], near_recv.at[1], rows=my_base + side)

    @pl.when(has_side)
    def _():
        to_side.start()

    def slot(s, p):
        return everyone.at[pl.ds((other_base + s) * per + p * piece, piece)]

    def arrive(s, p):
        send(slot(s, p), slot(s, p), first_send.at[p], slot_recv.at[s, p], rows=mate).wait_recv()

    def pass_on(s, p, send_sem, row):
        go(slot(s, p), slot(s, p), send_sem, slot_recv.at[s, p], rows=row)

    def arrive_column(column, h):
        ref = column_piece(column, h)
        send(ref, ref, col_send.at[0, h], col_recv.at[column, h], col=col_mate).wait_recv()

    eye = (
        lax.broadcasted_iota(jnp.int32, (width, order), 0) + q * width
        == lax.broadcasted_iota(jnp.int32, (width, order), 1)
    ).astype(F32)

    def prepare(i, carry):
        z_t = full[i]
        own = full[i, rows_of(q), :]
        square = (-0.5 * dot(z_t, z_t, TN)).astype(BF16)
        blocks = [v_near[i, k] for k in range(near)] + [v_cross[i, k] for k in range(cross)]
        wide = dot(square, jnp.concatenate(blocks, axis=1)).astype(BF16)
        for k in range(near + cross):
            g[i, k] = wide[:, k * order:(k + 1) * order]
        product = dot(own, v_diag[i], NT).astype(BF16)
        residual = (eye - dot(product, z_t, NT)).astype(BF16)
        w_diag[i] = (own.astype(F32) + 0.5 * dot(residual, z_t)).astype(BF16)
        return carry

    for t in range(parts + lag):
        if t < parts:
            arrive(m, t)
            for k, cousin in enumerate(cousins):
                pass_on(m, t, second_send.at[k, t], cousin)
            pass_on(m, t, third_send.at[0, t], mate)
        if 1 <= t <= len(halves):
            for k, column in enumerate(col_cousins):
                arrive_column(column, t - 1)
                ref = column_piece(column, t - 1)
                go(ref, ref, col_send.at[len(col_cousins) + 1 + k, t - 1], col_recv.at[column, t - 1], col=col_mate)
        if t == lag:
            own_full.wait()
            for load in loads:
                load.wait()
            for h in range(len(halves)):
                arrive_column(col_mate, h)
                for k in range(1, c // 2):
                    arrive_column((col_mate + 2 * k) % c, h)
        if t >= lag:
            for k in range(1, half // 2):
                s = (m + 2 * k) % half
                arrive(s, t - lag)
                pass_on(s, t - lag, third_send.at[k, t - lag], mate)
            lax.fori_loop((t - lag) * piece, (t - lag + 1) * piece, prepare, 0)

    own_all.wait()
    to_mate.wait_recv()

    @pl.when(has_side)
    def _():
        to_side.wait_recv()

    for p in range(parts):
        for k in range(half // 2):
            arrive((m + 1 - 2 * parity + 2 * k) % half, p)

    for copy in sent:
        copy.wait_send()

    @pl.when(has_side)
    def _():
        to_side.wait_send()


def finish_kernel(
    near_cols, cross_cols, everyone, g, w_diag, o_diag, o_near, o_cross, w_near, w_cross, diag_sem, out_sem,
):
    per, near = w_near.shape[:2]
    cross = w_cross.shape[1]
    out_diag = pltpu.make_async_copy(w_diag, o_diag, diag_sem.at[0])
    out_diag.start()

    def outs(i):
        return (
            pltpu.make_async_copy(w_near.at[i], o_near.at[i], out_sem.at[0, i]),
            pltpu.make_async_copy(w_cross.at[i], o_cross.at[i], out_sem.at[1, i]),
        )

    def finish(i, carry):
        for k in range(near):
            w_near[i, k] = dot(everyone[near_cols[k, i]], g[i, k], NT).astype(BF16)
        for k in range(cross):
            w_cross[i, k] = dot(everyone[cross_cols[k, i]], g[i, near + k], NT).astype(BF16)
        for copy in outs(i):
            copy.start()
        return carry

    lax.fori_loop(0, per, finish, 0)
    out_diag.wait()

    def drain(i, carry):
        for copy in outs(i):
            copy.wait()
        return carry

    lax.fori_loop(0, per, drain, 0)


def body(n, c, factor_t, intersection_diag, intersection_near, intersection_cross, near_cols, cross_cols):
    per, width, order = factor_t.shape
    near, cross = near_cols.shape[1], cross_cols.shape[1]
    half = n // 2
    parts = per // 2 if per % 2 == 0 else per
    col_parts = 2 if per % 2 == 0 else 1
    smem = pl.BlockSpec(memory_space=pltpu.SMEM)
    vmem = pl.BlockSpec(memory_space=pltpu.VMEM)
    hbm = pl.BlockSpec(memory_space=pl.ANY)
    dma = pltpu.SemaphoreType.DMA
    everyone, g, w_diag = pl.pallas_call(
        functools.partial(gather_kernel, n, c, parts, min(LAG, parts - 1)),
        out_shape=(
            pltpu.VMEM((n * per, width, order), BF16),
            pltpu.VMEM((per, near + cross, order, order), BF16),
            pltpu.VMEM((per, width, order), BF16),
        ),
        in_specs=[pl.BlockSpec(memory_space=pltpu.HBM)] * 4,
        out_specs=(vmem, vmem, vmem),
        scratch_shapes=[
            pltpu.VMEM((per, order, order), BF16),
            pltpu.VMEM(intersection_diag.shape, BF16),
            pltpu.VMEM(intersection_near.shape, BF16),
            pltpu.VMEM(intersection_cross.shape, BF16),
            dma((3,)),
            dma((2,)),
            dma((c, col_parts)),
            dma((c, col_parts)),
            dma((2,)),
            dma((2,)),
            dma((parts,)),
            dma((half, parts)),
            dma((half // 2, parts)),
            dma((half // 2, parts)),
        ],
        compiler_params=pltpu.CompilerParams(
            collective_id=0, has_side_effects=True, vmem_limit_bytes=VMEM_LIMIT,
        ),
    )(factor_t, intersection_diag, intersection_near, intersection_cross)
    return pl.pallas_call(
        finish_kernel,
        out_shape=(
            jax.ShapeDtypeStruct((per, width, order), BF16),
            jax.ShapeDtypeStruct((per, near, width, order), BF16),
            jax.ShapeDtypeStruct((per, cross, width, order), BF16),
        ),
        in_specs=[smem, smem, vmem, vmem, vmem],
        out_specs=(hbm, hbm, hbm),
        scratch_shapes=[
            pltpu.VMEM((per, near, width, order), BF16),
            pltpu.VMEM((per, cross, width, order), BF16),
            dma((1,)),
            dma((2, per)),
        ],
        compiler_params=pltpu.CompilerParams(vmem_limit_bytes=VMEM_LIMIT),
    )(near_cols.T, cross_cols.T, everyone, g, w_diag)


def solution(mesh):
    placed = (
        P("rows", "col", None),
        P("rows", None, None),
        P("rows", None, None, None),
        P("rows", None, None, None),
        P("rows", None),
        P("rows", None),
    )
    return jax.shard_map(
        functools.partial(body, mesh.shape["rows"], mesh.shape["col"]),
        mesh=mesh,
        in_specs=placed,
        out_specs=(
            P("rows", "col", None),
            P("rows", None, "col", None),
            P("rows", None, "col", None),
        ),
        check_vma=False,
    )
```

```python
import functools

import jax
import jax.numpy as jnp
from jax import lax
from jax.experimental import pallas as pl
from jax.experimental.pallas import tpu as pltpu
from jax.sharding import PartitionSpec as P

F32 = jnp.float32
BF16 = jnp.bfloat16
LAG = 5
VMEM_LIMIT = 16 * 1024 * 1024
VMEM_ALL = 67043328
SLACK = 96 * 1024
NT = (((1,), (1,)), ((), ()))
TN = (((0,), (0,)), ((), ()))


def dot(a, b, dims=(((1,), (0,)), ((), ()))):
    return lax.dot_general(a, b, dims, preferred_element_type=F32)


def split(rows, parts):
    size = rows // parts
    return [pl.ds(p * size, size) for p in range(parts)]


def gather_kernel(
    n, c, parts, lag,
    factor, s_diag, s_near, s_cross,
    everyone, g, w_diag,
    full, v_diag, v_near, v_cross,
    load_sem, own_sem, col_send, col_recv, near_send, near_recv,
    first_send, slot_recv, second_send, third_send,
):
    per, width, order = factor.shape
    near, cross = v_near.shape[1], v_cross.shape[1]
    half = n // 2
    piece = per // parts
    r = lax.axis_index("rows")
    q = lax.axis_index("col")
    upper = r // half
    m = r - upper * half
    my_base = upper * half
    other_base = (1 - upper) * half
    parity = m % 2
    mate = my_base + m + 1 - 2 * parity
    side = m - 1 + 2 * parity
    has_side = jnp.logical_and(side >= 0, side < half)
    partner = other_base + m
    cousins = [my_base + (m + 2 * k) % half for k in range(1, half // 2)]
    col_mate = q + 1 - 2 * (q % 2)
    col_cousins = [(q + 2 * k) % c for k in range(1, c // 2)]

    loads = [
        pltpu.make_async_copy(s_diag, v_diag, load_sem.at[0]),
        pltpu.make_async_copy(s_near, v_near, load_sem.at[1]),
        pltpu.make_async_copy(s_cross, v_cross, load_sem.at[2]),
    ]
    own_all = pltpu.make_async_copy(factor, everyone.at[pl.ds(r * per, per)], own_sem.at[0])

    def rows_of(column):
        return pl.ds(pl.multiple_of(column * width, width), width)

    own_full = pltpu.make_async_copy(factor, full.at[:, rows_of(q), :], own_sem.at[1])

    barrier = pltpu.get_barrier_semaphore()

    def greet(**where):
        pl.semaphore_signal(barrier, inc=1, device_id=where, device_id_type=pl.DeviceIdType.MESH)

    greet(rows=partner)
    greet(rows=mate)
    for cousin in cousins:
        greet(rows=cousin)
    greet(col=col_mate)
    for column in col_cousins:
        greet(col=column)

    @pl.when(has_side)
    def _():
        greet(rows=my_base + side)

    own_full.start()
    own_all.start()
    for load in loads:
        load.start()
    pl.semaphore_wait(barrier, 3 + len(cousins) + len(col_cousins) + has_side.astype(jnp.int32))

    def send(src, dst, send_sem, recv_sem, **where):
        return pltpu.make_async_remote_copy(
            src_ref=src, dst_ref=dst, send_sem=send_sem, recv_sem=recv_sem,
            device_id=where, device_id_type=pl.DeviceIdType.MESH,
        )

    sent = []

    def go(*args, **where):
        copy = send(*args, **where)
        copy.start()
        sent.append(copy)
        return copy

    for p in range(parts):
        go(
            factor.at[pl.ds(p * piece, piece)],
            everyone.at[pl.ds(r * per + p * piece, piece)],
            first_send.at[p], slot_recv.at[m, p], rows=partner,
        )
    halves = split(per, col_recv.shape[1])

    def column_piece(column, h):
        return full.at[halves[h], rows_of(column), :]

    for h in range(len(halves)):
        for k, column in enumerate(col_cousins):
            go(factor.at[halves[h]], column_piece(q, h), col_send.at[k, h], col_recv.at[q, h], col=column)
        go(factor.at[halves[h]], column_piece(q, h), col_send.at[len(col_cousins), h], col_recv.at[q, h], col=col_mate)
    mine = everyone.at[pl.ds(r * per, per)]
    to_mate = go(factor, mine, near_send.at[0], near_recv.at[0], rows=mate)
    to_side = send(factor, mine, near_send.at[1], near_recv.at[1], rows=my_base + side)

    @pl.when(has_side)
    def _():
        to_side.start()

    def slot(s, p):
        return everyone.at[pl.ds((other_base + s) * per + p * piece, piece)]

    def arrive(s, p):
        send(slot(s, p), slot(s, p), first_send.at[p], slot_recv.at[s, p], rows=mate).wait_recv()

    def pass_on(s, p, send_sem, row):
        go(slot(s, p), slot(s, p), send_sem, slot_recv.at[s, p], rows=row)

    def arrive_column(column, h):
        ref = column_piece(column, h)
        send(ref, ref, col_send.at[0, h], col_recv.at[column, h], col=col_mate).wait_recv()

    eye = (
        lax.broadcasted_iota(jnp.int32, (width, order), 0) + q * width
        == lax.broadcasted_iota(jnp.int32, (width, order), 1)
    ).astype(F32)

    def prepare(i, carry):
        z_t = full[i]
        own = full[i, rows_of(q), :]
        square = (-0.5 * dot(z_t, z_t, TN)).astype(BF16)
        blocks = [v_near[i, k] for k in range(near)] + [v_cross[i, k] for k in range(cross)]
        wide = dot(square, jnp.concatenate(blocks, axis=1)).astype(BF16)
        for k in range(near + cross):
            g[i, k] = wide[:, k * order:(k + 1) * order]
        product = dot(own, v_diag[i], NT).astype(BF16)
        residual = (eye - dot(product, z_t, NT)).astype(BF16)
        w_diag[i] = (own.astype(F32) + 0.5 * dot(residual, z_t)).astype(BF16)
        return carry

    for t in range(parts + lag):
        if t < parts:
            arrive(m, t)
            for k, cousin in enumerate(cousins):
                pass_on(m, t, second_send.at[k, t], cousin)
            pass_on(m, t, third_send.at[0, t], mate)
        if 1 <= t <= len(halves):
            for k, column in enumerate(col_cousins):
                arrive_column(column, t - 1)
                ref = column_piece(column, t - 1)
                go(ref, ref, col_send.at[len(col_cousins) + 1 + k, t - 1], col_recv.at[column, t - 1], col=col_mate)
        if t == lag:
            own_full.wait()
            for load in loads:
                load.wait()
            for h in range(len(halves)):
                arrive_column(col_mate, h)
                for k in range(1, c // 2):
                    arrive_column((col_mate + 2 * k) % c, h)
        if t >= lag:
            for k in range(1, half // 2):
                s = (m + 2 * k) % half
                arrive(s, t - lag)
                pass_on(s, t - lag, third_send.at[k, t - lag], mate)
            lax.fori_loop((t - lag) * piece, (t - lag + 1) * piece, prepare, 0)

    own_all.wait()
    to_mate.wait_recv()

    @pl.when(has_side)
    def _():
        to_side.wait_recv()

    for p in range(parts):
        for k in range(half // 2):
            arrive((m + 1 - 2 * parity + 2 * k) % half, p)

    for copy in sent:
        copy.wait_send()

    @pl.when(has_side)
    def _():
        to_side.wait_send()


def finish_kernel(
    near_cols, cross_cols, everyone, g, w_diag, o_diag, o_near, o_cross, w_near, w_cross, diag_sem, out_sem,
):
    per, near = w_near.shape[:2]
    cross = w_cross.shape[1]
    out_diag = pltpu.make_async_copy(w_diag, o_diag, diag_sem.at[0])
    out_diag.start()

    def outs(i):
        return (
            pltpu.make_async_copy(w_near.at[i], o_near.at[i], out_sem.at[0, i]),
            pltpu.make_async_copy(w_cross.at[i], o_cross.at[i], out_sem.at[1, i]),
        )

    def finish(i, carry):
        for k in range(near):
            w_near[i, k] = dot(everyone[near_cols[k, i]], g[i, k], NT).astype(BF16)
        for k in range(cross):
            w_cross[i, k] = dot(everyone[cross_cols[k, i]], g[i, near + k], NT).astype(BF16)
        for copy in outs(i):
            copy.start()
        return carry

    lax.fori_loop(0, per, finish, 0)
    out_diag.wait()

    def drain(i, carry):
        for copy in outs(i):
            copy.wait()
        return carry

    lax.fori_loop(0, per, drain, 0)


def body(n, c, factor_t, intersection_diag, intersection_near, intersection_cross, near_cols, cross_cols):
    per, width, order = factor_t.shape
    near, cross = near_cols.shape[1], cross_cols.shape[1]
    half = n // 2
    parts = per // 2 if per % 2 == 0 else per
    col_parts = 2 if per % 2 == 0 else 1
    smem = pl.BlockSpec(memory_space=pltpu.SMEM)
    vmem = pl.BlockSpec(memory_space=pltpu.VMEM)
    hbm = pl.BlockSpec(memory_space=pl.ANY)
    dma = pltpu.SemaphoreType.DMA
    kept = 2 * order * (n * per * width + per * (near + cross) * order + per * width)
    everyone, g, w_diag = pl.pallas_call(
        functools.partial(gather_kernel, n, c, parts, min(LAG, parts - 1)),
        out_shape=(
            pltpu.VMEM((n * per, width, order), BF16),
            pltpu.VMEM((per, near + cross, order, order), BF16),
            pltpu.VMEM((per, width, order), BF16),
        ),
        in_specs=[pl.BlockSpec(memory_space=pltpu.HBM)] * 4,
        out_specs=(vmem, vmem, vmem),
        scratch_shapes=[
            pltpu.VMEM((per, order, order), BF16),
            pltpu.VMEM(intersection_diag.shape, BF16),
            pltpu.VMEM(intersection_near.shape, BF16),
            pltpu.VMEM(intersection_cross.shape, BF16),
            dma((3,)),
            dma((2,)),
            dma((c, col_parts)),
            dma((c, col_parts)),
            dma((2,)),
            dma((2,)),
            dma((parts,)),
            dma((half, parts)),
            dma((half // 2, parts)),
            dma((half // 2, parts)),
        ],
        compiler_params=pltpu.CompilerParams(
            collective_id=0, has_side_effects=True, vmem_limit_bytes=VMEM_ALL - kept - SLACK,
        ),
    )(factor_t, intersection_diag, intersection_near, intersection_cross)
    return pl.pallas_call(
        finish_kernel,
        out_shape=(
            jax.ShapeDtypeStruct((per, width, order), BF16),
            jax.ShapeDtypeStruct((per, near, width, order), BF16),
            jax.ShapeDtypeStruct((per, cross, width, order), BF16),
        ),
        in_specs=[smem, smem, vmem, vmem, vmem],
        out_specs=(hbm, hbm, hbm),
        scratch_shapes=[
            pltpu.VMEM((per, near, width, order), BF16),
            pltpu.VMEM((per, cross, width, order), BF16),
            dma((1,)),
            dma((2, per)),
        ],
        compiler_params=pltpu.CompilerParams(vmem_limit_bytes=VMEM_LIMIT),
    )(near_cols.T, cross_cols.T, everyone, g, w_diag)


def solution(mesh):
    placed = (
        P("rows", "col", None),
        P("rows", None, None),
        P("rows", None, None, None),
        P("rows", None, None, None),
        P("rows", None),
        P("rows", None),
    )
    return jax.shard_map(
        functools.partial(body, mesh.shape["rows"], mesh.shape["col"]),
        mesh=mesh,
        in_specs=placed,
        out_specs=(
            P("rows", "col", None),
            P("rows", None, "col", None),
            P("rows", None, "col", None),
        ),
        check_vma=False,
    )
```

```python
import functools

import jax
import jax.numpy as jnp
from jax import lax
from jax.experimental import pallas as pl
from jax.experimental.pallas import tpu as pltpu
from jax.sharding import PartitionSpec as P

F32 = jnp.float32
BF16 = jnp.bfloat16
LAG = 2
PARTS = 2
VMEM_LIMIT = 16 * 1024 * 1024
VMEM_ALL = 67043328
SLACK = 96 * 1024
NT = (((1,), (1,)), ((), ()))
TN = (((0,), (0,)), ((), ()))


def dot(a, b, dims=(((1,), (0,)), ((), ()))):
    return lax.dot_general(a, b, dims, preferred_element_type=F32)


def split(rows, parts):
    size = rows // parts
    return [pl.ds(p * size, size) for p in range(parts)]


def gather_kernel(
    n, c, parts, lag,
    factor, s_diag, s_near, s_cross,
    everyone, g, w_diag,
    full, v_diag, v_near, v_cross,
    load_sem, own_sem, col_send, col_recv, near_send, near_recv,
    first_send, slot_recv, second_send, third_send,
):
    per, width, order = factor.shape
    near, cross = v_near.shape[1], v_cross.shape[1]
    half = n // 2
    cut = [per * p // parts for p in range(parts + 1)]
    r = lax.axis_index("rows")
    q = lax.axis_index("col")
    upper = r // half
    m = r - upper * half
    my_base = upper * half
    other_base = (1 - upper) * half
    parity = m % 2
    mate = my_base + m + 1 - 2 * parity
    side = m - 1 + 2 * parity
    has_side = jnp.logical_and(side >= 0, side < half)
    partner = other_base + m
    cousins = [my_base + (m + 2 * k) % half for k in range(1, half // 2)]
    col_mate = q + 1 - 2 * (q % 2)
    col_cousins = [(q + 2 * k) % c for k in range(1, c // 2)]

    loads = [
        pltpu.make_async_copy(s_diag, v_diag, load_sem.at[0]),
        pltpu.make_async_copy(s_near, v_near, load_sem.at[1]),
        pltpu.make_async_copy(s_cross, v_cross, load_sem.at[2]),
    ]
    own_all = pltpu.make_async_copy(factor, everyone.at[pl.ds(r * per, per)], own_sem.at[0])

    def rows_of(column):
        return pl.ds(pl.multiple_of(column * width, width), width)

    own_full = pltpu.make_async_copy(factor, full.at[:, rows_of(q), :], own_sem.at[1])

    barrier = pltpu.get_barrier_semaphore()

    def greet(**where):
        pl.semaphore_signal(barrier, inc=1, device_id=where, device_id_type=pl.DeviceIdType.MESH)

    greet(rows=partner)
    greet(rows=mate)
    for cousin in cousins:
        greet(rows=cousin)
    greet(col=col_mate)
    for column in col_cousins:
        greet(col=column)

    @pl.when(has_side)
    def _():
        greet(rows=my_base + side)

    own_full.start()
    own_all.start()
    for load in loads:
        load.start()
    pl.semaphore_wait(barrier, 3 + len(cousins) + len(col_cousins) + has_side.astype(jnp.int32))

    def send(src, dst, send_sem, recv_sem, **where):
        return pltpu.make_async_remote_copy(
            src_ref=src, dst_ref=dst, send_sem=send_sem, recv_sem=recv_sem,
            device_id=where, device_id_type=pl.DeviceIdType.MESH,
        )

    sent = []

    def go(*args, **where):
        copy = send(*args, **where)
        copy.start()
        sent.append(copy)
        return copy

    for p in range(parts):
        go(
            factor.at[pl.ds(cut[p], cut[p + 1] - cut[p])],
            everyone.at[pl.ds(r * per + cut[p], cut[p + 1] - cut[p])],
            first_send.at[p], slot_recv.at[m, p], rows=partner,
        )
    halves = split(per, col_recv.shape[1])

    def column_piece(column, h):
        return full.at[halves[h], rows_of(column), :]

    for h in range(len(halves)):
        for k, column in enumerate(col_cousins):
            go(factor.at[halves[h]], column_piece(q, h), col_send.at[k, h], col_recv.at[q, h], col=column)
        go(factor.at[halves[h]], column_piece(q, h), col_send.at[len(col_cousins), h], col_recv.at[q, h], col=col_mate)
    mine = everyone.at[pl.ds(r * per, per)]
    to_mate = go(factor, mine, near_send.at[0], near_recv.at[0], rows=mate)
    to_side = send(factor, mine, near_send.at[1], near_recv.at[1], rows=my_base + side)

    @pl.when(has_side)
    def _():
        to_side.start()

    def slot(s, p):
        return everyone.at[pl.ds((other_base + s) * per + cut[p], cut[p + 1] - cut[p])]

    def arrive(s, p):
        send(slot(s, p), slot(s, p), first_send.at[p], slot_recv.at[s, p], rows=mate).wait_recv()

    def pass_on(s, p, send_sem, row):
        go(slot(s, p), slot(s, p), send_sem, slot_recv.at[s, p], rows=row)

    def arrive_column(column, h):
        ref = column_piece(column, h)
        send(ref, ref, col_send.at[0, h], col_recv.at[column, h], col=col_mate).wait_recv()

    eye = (
        lax.broadcasted_iota(jnp.int32, (width, order), 0) + q * width
        == lax.broadcasted_iota(jnp.int32, (width, order), 1)
    ).astype(F32)

    def prepare(i, carry):
        z_t = full[i]
        own = full[i, rows_of(q), :]
        square = (-0.5 * dot(z_t, z_t, TN)).astype(BF16)
        blocks = [v_near[i, k] for k in range(near)] + [v_cross[i, k] for k in range(cross)]
        wide = dot(square, jnp.concatenate(blocks, axis=1)).astype(BF16)
        for k in range(near + cross):
            g[i, k] = wide[:, k * order:(k + 1) * order]
        product = dot(own, v_diag[i], NT).astype(BF16)
        residual = (eye - dot(product, z_t, NT)).astype(BF16)
        w_diag[i] = (own.astype(F32) + 0.5 * dot(residual, z_t)).astype(BF16)
        return carry

    for t in range(parts + lag):
        if t < parts:
            arrive(m, t)
            for k, cousin in enumerate(cousins):
                pass_on(m, t, second_send.at[k, t], cousin)
            pass_on(m, t, third_send.at[0, t], mate)
        if 1 <= t <= len(halves):
            for k, column in enumerate(col_cousins):
                arrive_column(column, t - 1)
                ref = column_piece(column, t - 1)
                go(ref, ref, col_send.at[len(col_cousins) + 1 + k, t - 1], col_recv.at[column, t - 1], col=col_mate)
        if t == lag:
            own_full.wait()
            for load in loads:
                load.wait()
            for h in range(len(halves)):
                arrive_column(col_mate, h)
                for k in range(1, c // 2):
                    arrive_column((col_mate + 2 * k) % c, h)
        if t >= lag:
            for k in range(1, half // 2):
                s = (m + 2 * k) % half
                arrive(s, t - lag)
                pass_on(s, t - lag, third_send.at[k, t - lag], mate)
            lax.fori_loop(cut[t - lag], cut[t - lag + 1], prepare, 0, unroll=True)

    own_all.wait()
    to_mate.wait_recv()

    @pl.when(has_side)
    def _():
        to_side.wait_recv()

    for p in range(parts):
        for k in range(half // 2):
            arrive((m + 1 - 2 * parity + 2 * k) % half, p)

    for copy in sent:
        copy.wait_send()

    @pl.when(has_side)
    def _():
        to_side.wait_send()


def finish_kernel(
    near_cols, cross_cols, everyone, g, w_diag, o_diag, o_near, o_cross, w_near, w_cross, diag_sem, out_sem,
):
    per, near = w_near.shape[:2]
    cross = w_cross.shape[1]
    out_diag = pltpu.make_async_copy(w_diag, o_diag, diag_sem.at[0])
    out_diag.start()

    def outs(i):
        return (
            pltpu.make_async_copy(w_near.at[i], o_near.at[i], out_sem.at[0, i]),
            pltpu.make_async_copy(w_cross.at[i], o_cross.at[i], out_sem.at[1, i]),
        )

    def finish(i, carry):
        for k in range(near):
            w_near[i, k] = dot(everyone[near_cols[k, i]], g[i, k], NT).astype(BF16)
        for k in range(cross):
            w_cross[i, k] = dot(everyone[cross_cols[k, i]], g[i, near + k], NT).astype(BF16)
        for copy in outs(i):
            copy.start()
        return carry

    lax.fori_loop(0, per, finish, 0, unroll=True)
    out_diag.wait()

    def drain(i, carry):
        for copy in outs(i):
            copy.wait()
        return carry

    lax.fori_loop(0, per, drain, 0)


def body(n, c, factor_t, intersection_diag, intersection_near, intersection_cross, near_cols, cross_cols):
    per, width, order = factor_t.shape
    near, cross = near_cols.shape[1], cross_cols.shape[1]
    half = n // 2
    parts = min(PARTS, per)
    col_parts = 2 if per % 2 == 0 else 1
    smem = pl.BlockSpec(memory_space=pltpu.SMEM)
    vmem = pl.BlockSpec(memory_space=pltpu.VMEM)
    hbm = pl.BlockSpec(memory_space=pl.ANY)
    dma = pltpu.SemaphoreType.DMA
    kept = 2 * order * (n * per * width + per * (near + cross) * order + per * width)
    everyone, g, w_diag = pl.pallas_call(
        functools.partial(gather_kernel, n, c, parts, LAG),
        out_shape=(
            pltpu.VMEM((n * per, width, order), BF16),
            pltpu.VMEM((per, near + cross, order, order), BF16),
            pltpu.VMEM((per, width, order), BF16),
        ),
        in_specs=[pl.BlockSpec(memory_space=pltpu.HBM)] * 4,
        out_specs=(vmem, vmem, vmem),
        scratch_shapes=[
            pltpu.VMEM((per, order, order), BF16),
            pltpu.VMEM(intersection_diag.shape, BF16),
            pltpu.VMEM(intersection_near.shape, BF16),
            pltpu.VMEM(intersection_cross.shape, BF16),
            dma((3,)),
            dma((2,)),
            dma((c, col_parts)),
            dma((c, col_parts)),
            dma((2,)),
            dma((2,)),
            dma((parts,)),
            dma((half, parts)),
            dma((half // 2, parts)),
            dma((half // 2, parts)),
        ],
        compiler_params=pltpu.CompilerParams(
            collective_id=0, has_side_effects=True, vmem_limit_bytes=VMEM_ALL - kept - SLACK,
        ),
    )(factor_t, intersection_diag, intersection_near, intersection_cross)
    return pl.pallas_call(
        finish_kernel,
        out_shape=(
            jax.ShapeDtypeStruct((per, width, order), BF16),
            jax.ShapeDtypeStruct((per, near, width, order), BF16),
            jax.ShapeDtypeStruct((per, cross, width, order), BF16),
        ),
        in_specs=[smem, smem, vmem, vmem, vmem],
        out_specs=(hbm, hbm, hbm),
        scratch_shapes=[
            pltpu.VMEM((per, near, width, order), BF16),
            pltpu.VMEM((per, cross, width, order), BF16),
            dma((1,)),
            dma((2, per)),
        ],
        compiler_params=pltpu.CompilerParams(vmem_limit_bytes=VMEM_LIMIT),
    )(near_cols.T, cross_cols.T, everyone, g, w_diag)


def solution(mesh):
    placed = (
        P("rows", "col", None),
        P("rows", None, None),
        P("rows", None, None, None),
        P("rows", None, None, None),
        P("rows", None),
        P("rows", None),
    )
    return jax.shard_map(
        functools.partial(body, mesh.shape["rows"], mesh.shape["col"]),
        mesh=mesh,
        in_specs=placed,
        out_specs=(
            P("rows", "col", None),
            P("rows", None, "col", None),
            P("rows", None, "col", None),
        ),
        check_vma=False,
    )
```
